32 devices in a mesh: seg: 8 (over y, x, core), slab: 4 (over z).
Axes of the slice: x: 2, y: 2, z: 4, core: 2. Of those that a mesh axis runs over, the one named last changes fastest.
Arguments:
- mismatch: float32 [8, 128, 32, 128], P('seg', 'slab'), may hold values from -60 to 60, as said below
- advect: float32 [8, 128, 32, 128], P('seg', 'slab'), may hold values from 0.1 to 0.7
- damping: float32 [8, 128, 32, 128], P('seg', 'slab'), may hold values from 0 to 0.2
- axial_shift: int32 [1], replicated, may hold values from 1 to 31
- radius: float32 [1], replicated, may hold values from 0.5 to 2
Outputs:
- step: float32 [8, 128, 32, 128], P('seg', 'slab')
- hessenberg: float32 [3, 2], replicated
The draws below stay inside these ranges and needn't reach their ends.
Inputs may be any that keep to these rules, and one draw needn't show every extreme that they name: mismatch is finite and of order one to ten.
All inputs are finite; a program needn't handle non-finite values.
Results may differ from the reference program's by a relative error of at most 0.00012.
Values sent between devices are 32-bit elements; how exact they have to be, the bound alone decides.
A program may use at most 64 MiB of HBM per device.

```python
import math
import jax
import jax.numpy as jnp
from jax import lax

AXL = 32
NR = 32
NT = 128
STEPS = 8
KRY = 2
SEGMENTS = 8
NZ = 128


LOG_THREE = math.log(3.0)


def draw_mismatch(key, part):
    shape = (SEGMENTS, NZ, NR, NT)
    seg_ramp = jnp.arange(SEGMENTS, dtype=jnp.float32) / max(SEGMENTS - 1, 1)
    axial_ramp = jnp.arange(NZ, dtype=jnp.float32) / max(NZ - 1, 1)
    scaling = jnp.exp(LOG_THREE * seg_ramp)[:, None, None, None] * jnp.exp(LOG_THREE * axial_ramp)[None, :, None, None]
    first_key = jax.random.fold_in(key, 0)
    base = jnp.clip(jax.random.normal(first_key, shape, jnp.float32), -6.0, 6.0)
    return (base * scaling).astype(jnp.float32)


def level_of(stream_key, extent, pieces, least, top_value):
    factor_of, own = 1.0, jax.random.fold_in(stream_key, 6)
    for position, blocks in pieces:
        heights = jnp.exp(jax.random.uniform(jax.random.fold_in(own, position), (blocks,), jnp.float32, least / len(pieces), top_value / len(pieces)))
        factor_of = factor_of * jnp.repeat(heights, extent[position] // blocks).reshape([-1 if axis == position else 1 for axis in range(len(extent))])
    return factor_of


def setup_inputs(seed: int = 0) -> dict:
    key_list = jax.random.split(jax.random.key(seed), 6)
    mismatch = draw_mismatch(jax.random.fold_in(key_list[5], 71), 0)
    advect = jnp.clip(0.1 + 0.59999999 * jax.random.uniform(key_list[1], (SEGMENTS, NZ, NR, NT), jnp.float32) ** level_of(key_list[1], (SEGMENTS, NZ, NR, NT), ((0, 8), (1, 4)), -0.2, 0.2), 0.1, 0.7)
    damping = jnp.clip(0.2 * jax.random.uniform(key_list[2], (SEGMENTS, NZ, NR, NT), jnp.float32) ** level_of(key_list[2], (SEGMENTS, NZ, NR, NT), ((0, 8), (1, 4)), -0.2, 0.2), 0.0, 0.2)
    axial_shift = jax.random.randint(key_list[3], (1,), 1, AXL).astype(jnp.int32)
    radius = jnp.clip(jnp.exp(jax.random.uniform(key_list[4], (1,), jnp.float32, math.log(0.5), math.log(2.0))), 0.5, 2.0)
    return dict(mismatch=mismatch, advect=advect, damping=damping, axial_shift=axial_shift, radius=radius)


KAPPA = 0.15

def advance(centre, z_ahead, z_behind, advect, damping):
    wall_zero = jnp.zeros_like(centre[..., :1, :])
    r_outer = jnp.concatenate([centre[..., 1:, :], wall_zero], axis=-2)
    r_inner = jnp.concatenate([wall_zero, centre[..., :-1, :]], axis=-2)
    t_ahead = jnp.roll(centre, -1, axis=-1)
    t_behind = jnp.roll(centre, 1, axis=-1)
    return centre + KAPPA * (z_ahead + z_behind + r_outer + r_inner + t_ahead + t_behind - 6.0 * centre) - 0.5 * advect * (z_ahead - z_behind) - damping * centre

def propagate(triple):
    current, advect, damping = triple
    for repeat in range(STEPS):
        current = advance(current, jnp.roll(current, -1, axis=0), jnp.roll(current, 1, axis=0), advect, damping)
    return current

def jacobian(direction, advect, damping, axial_shift):
    flowed = lax.map(propagate, (direction, advect, damping))
    following = jnp.roll(direction, -1, axis=0)
    wrapped = jnp.roll(direction[0], axial_shift[0], axis=0)
    following = following.at[-1].set(wrapped)
    return flowed - following

def hookstep(hessenberg, rhs_norm, radius):
    normal = jnp.dot(hessenberg.T, hessenberg, precision=lax.Precision.HIGHEST)
    normal = normal + jnp.eye(KRY, dtype=jnp.float32) / (radius[0] * radius[0])
    target = rhs_norm * hessenberg[0]
    factor = jnp.linalg.cholesky(normal)
    forward = []
    for pivot in range(KRY):
        running = target[pivot]
        for across in range(pivot):
            running = running - factor[pivot, across] * forward[across]
        forward.append(running / factor[pivot, pivot])
    result = [None] * KRY
    for pivot in reversed(range(KRY)):
        running = forward[pivot]
        for across in range(pivot + 1, KRY):
            running = running - factor[across, pivot] * result[across]
        result[pivot] = running / factor[pivot, pivot]
    return result

def reference(mismatch, advect, damping, axial_shift, radius):
    rhs_norm = jnp.sqrt(jnp.sum(mismatch * mismatch))
    krylov = [mismatch / rhs_norm]
    columns = []
    for column in range(KRY):
        image = jacobian(krylov[column], advect, damping, axial_shift)
        projected = jnp.stack([jnp.sum(vector * image) for vector in krylov])
        for member in range(column + 1):
            image = image - projected[member] * krylov[member]
        new_norm = jnp.sqrt(jnp.sum(image * image))
        columns.append(jnp.concatenate([projected, new_norm[None], jnp.zeros((KRY - column - 1,), jnp.float32)]))
        krylov.append(image / new_norm)
    hessenberg = jnp.stack(columns, axis=1)
    weights = hookstep(hessenberg, rhs_norm, radius)
    step = weights[0] * krylov[0]
    for member in range(1, KRY):
        step = step + weights[member] * krylov[member]
    return (step, hessenberg)
```

```python
import functools

import jax
import jax.numpy as jnp
from jax import lax
from jax.experimental import pallas as pl
from jax.experimental.pallas import tpu as pltpu
from jax.sharding import PartitionSpec as P

STEPS = 8
KRY = 2
KAPPA = 0.15
WIDTH = 8

MESH = pl.DeviceIdType.MESH


def stencil(behind, centre, ahead, advect, damping):
    blocks, rows, lanes = centre.shape
    row = lax.broadcasted_iota(jnp.int32, centre.shape, 1)
    wall = jnp.zeros((1, rows, lanes), jnp.float32)
    around = pltpu.roll(centre, 1, 2) + pltpu.roll(centre, lanes - 1, 2)
    down = pltpu.roll(centre, 1, 1)
    up = pltpu.roll(centre, rows - 1, 1)
    inner = jnp.where(row == 0, jnp.concatenate([wall, down[:-1]], axis=0), down)
    outer = jnp.where(row == rows - 1, jnp.concatenate([up[1:], wall], axis=0), up)
    total = (around + (inner + outer)) + (ahead + behind)
    return centre * ((1.0 - 6.0 * KAPPA) - damping) + KAPPA * total + (0.5 * advect) * (behind - ahead)


def krylov_kernel(
    seg_n, slab_n, width,
    shift_ref, p_ref, a_ref, g_ref,
    p1_ref, totals_ref,
    levels, adv, dam, next_a, next_b, seg_sums, slab_sums,
    load_sem, halo_send, halo_recv, pair_send, pair_recv, cross_send, cross_recv,
    out_sem, seg_send, seg_recv, slab_send, slab_recv,
):
    loc = p_ref.shape[0]
    full = loc + 2 * width
    seg = lax.axis_index("seg")
    slab = lax.axis_index("slab")
    at = lambda s, z: {"seg": lax.rem(seg + s, seg_n), "slab": lax.rem(slab + z, slab_n)}
    coupled = (next_a, next_b)

    barrier = pltpu.get_barrier_semaphore()
    peers = [(0, z) for z in range(1, slab_n)] + [(s, 0) for s in range(1, seg_n)]
    peers += [(seg_n - 1, 1), (1, slab_n - 1)]
    for s, z in peers:
        pl.semaphore_signal(barrier, inc=1, device_id=at(s, z), device_id_type=MESH)
    own = pl.ds(width, loc)
    loads = [
        pltpu.make_async_copy(p_ref, levels.at[0, own], load_sem.at[0]),
        pltpu.make_async_copy(a_ref, adv.at[own], load_sem.at[1]),
        pltpu.make_async_copy(g_ref, dam.at[own], load_sem.at[2]),
    ]
    for load in loads:
        load.start()

    def halo(source, first, target, count, place):
        return [
            pltpu.make_async_remote_copy(
                src_ref=source.at[pl.ds(first + loc - count, count)],
                dst_ref=target.at[pl.ds(width - count, count)],
                send_sem=halo_send.at[place, 0], recv_sem=halo_recv.at[place, 0],
                device_id=at(0, 1), device_id_type=MESH,
            ),
            pltpu.make_async_remote_copy(
                src_ref=source.at[pl.ds(first, count)],
                dst_ref=target.at[pl.ds(width + loc, count)],
                send_sem=halo_send.at[place, 1], recv_sem=halo_recv.at[place, 1],
                device_id=at(0, slab_n - 1), device_id_type=MESH,
            ),
        ]

    def pair(source, column):
        return pltpu.make_async_remote_copy(
            src_ref=source, dst_ref=coupled[column].at[pl.ds(loc, loc)],
            send_sem=pair_send.at[column], recv_sem=pair_recv.at[column],
            device_id=at(seg_n - 1, 0), device_id_type=MESH,
        )

    def cross(source, column):
        return pltpu.make_async_remote_copy(
            src_ref=source, dst_ref=coupled[column].at[pl.ds(0, loc)],
            send_sem=cross_send.at[column], recv_sem=cross_recv.at[column],
            device_id=at(seg_n - 1, 1), device_id_type=MESH,
        )

    def sweep(level, start, count):
        before = levels[level, start - 1]
        here = levels[level, start]
        for plane in range(count):
            after = levels[level, start + plane + 1]
            levels[level + 1, start + plane] = stencil(
                before, here, after, adv[start + plane], dam[start + plane]
            )
            before, here = here, after

    thirds = -(-(loc - 2) // 3)

    def interior(base):
        def one(k, carry):
            def piece(i, inner):
                sweep(base + k, width + k + 1 + (i * (loc - 2 - 2 * k - thirds)) // 2, thirds)
                return inner
            return lax.fori_loop(0, 3, piece, carry)
        lax.fori_loop(0, width, one, 0)

    def edges(base):
        def one(k, carry):
            sweep(base + k, k + 1, width)
            sweep(base + k, full - 1 - k - width, width)
            return carry
        lax.fori_loop(0, width, one, 0)

    pl.semaphore_wait(barrier, len(peers))
    exchanges = KRY * STEPS // width
    sent = halo(p_ref, 0, levels.at[0], width, 0)
    sent += halo(a_ref, 0, adv, width - 1, exchanges)
    sent += halo(g_ref, 0, dam, width - 1, exchanges + 1)
    for copy in sent:
        copy.start()
    pair(p_ref, 0).start()

    @pl.when(seg == 0)
    def _():
        cross(p_ref, 0).start()

    for load in loads:
        load.wait()

    zero = jnp.zeros(p_ref.shape[1:], jnp.float32)
    offset = jnp.where(seg == seg_n - 1, loc - shift_ref[0], loc)
    sums = []
    for column in range(KRY):
        source = p_ref if column == 0 else levels.at[STEPS, own]
        for part in range(STEPS // width):
            base = column * STEPS + part * width
            if base > 0:
                sent = halo(levels.at[base], width, levels.at[base], width, base // width)
                for copy in sent:
                    copy.start()
                if part == 0:
                    pair(source, column).start()

                    @pl.when(seg == 0)
                    def _():
                        cross(source, column).start()

            interior(base)
            for copy in sent:
                copy.wait()
            edges(base)
        pair(source, column).wait()

        @pl.when(seg == 0)
        def _():
            cross(source, column).wait_send()

        @pl.when(seg == seg_n - 1)
        def _():
            cross(source, column).wait_recv()

        last = (column + 1) * STEPS

        def couple(i, acc):
            image = levels[last, width + i] - coupled[column][offset + i]
            if column == 0:
                levels[last, width + i] = image
            first = levels[0, width + i]
            second = image if column == 0 else levels[STEPS, width + i]
            head = first * first if column == 0 else first * image
            mid = first * image if column == 0 else second * image
            return (acc[0] + head, acc[1] + mid, acc[2] + image * image)

        def couple_group(i, acc):
            for j in range(4):
                acc = couple(4 * i + j, acc)
            return acc

        sums += lax.fori_loop(0, loc // 4, couple_group, (zero, zero, zero))
        if column == 0:
            store = pltpu.make_async_copy(levels.at[STEPS, own], p1_ref, out_sem)
            store.start()

    lane = lax.broadcasted_iota(jnp.int32, (1, zero.shape[-1]), 1)
    row = jnp.zeros(lane.shape, jnp.float32)
    for place, entry in enumerate(sums):
        value = jnp.sum(jnp.sum(entry, axis=0), axis=(0, 1), keepdims=True)
        row = row + jnp.where(lane == place, value, 0.0)

    def share(row, buffer, me, count, where, send, recv):
        buffer[me] = row
        copies = []
        for d in range(1, count):
            copies.append(
                pltpu.make_async_remote_copy(
                    src_ref=buffer.at[me], dst_ref=buffer.at[me],
                    send_sem=send.at[d - 1], recv_sem=recv.at[d - 1],
                    device_id=where(d), device_id_type=MESH,
                )
            )
        for copy in copies:
            copy.start()
        for copy in copies:
            copy.wait()
        total = buffer[0]
        for d in range(1, count):
            total = total + buffer[d]
        return total

    row = share(row, seg_sums, seg, seg_n, lambda d: at(d, 0), seg_send, seg_recv)
    row = share(row, slab_sums, slab, slab_n, lambda d: at(0, d), slab_send, slab_recv)
    totals_ref[...] = row
    store.wait()


def step_kernel(radius_ref, totals_ref, p0_ref, p1_ref, step_ref, hess_ref, x0, x1, y, in_sem, out_sem):
    loc = p0_ref.shape[0]
    parts = 4
    size = loc // parts
    pieces = [pl.ds(i * size, size) for i in range(parts)]
    loads = []
    for i, piece in enumerate(pieces):
        loads.append(
            (
                pltpu.make_async_copy(p0_ref.at[piece], x0.at[piece], in_sem.at[0, i]),
                pltpu.make_async_copy(p1_ref.at[piece], x1.at[piece], in_sem.at[1, i]),
            )
        )
    for pair in loads:
        for load in pair:
            load.start()

    totals = totals_ref[...]
    lane = lax.broadcasted_iota(jnp.int32, totals.shape, 1)
    entry = lambda i: jnp.sum(jnp.where(lane == i, totals, 0.0), axis=1, keepdims=True)
    g00, g01, g11, g02, g12, g22 = [jnp.broadcast_to(entry(i), totals.shape) for i in range(6)]
    gram = ((g00, g01, g02), (g01, g11, g12), (g02, g12, g22))

    def form(left, right):
        total = None
        for i, a in left.items():
            inner = None
            for j, b in right.items():
                term = gram[i][j] * b
                inner = term if inner is None else inner + term
            total = a * inner if total is None else total + a * inner
        return total

    norm = jnp.sqrt(g00)
    v0 = {0: 1.0 / norm}
    image = {1: v0[0]}
    h00 = form(v0, image)
    image = {0: -h00 * v0[0], 1: image[1]}
    h10 = jnp.sqrt(form(image, image))
    v1 = {0: image[0] / h10, 1: image[1] / h10}
    image = {1: v1[0], 2: v1[1]}
    h01 = form(v0, image)
    h11 = form(v1, image)
    image = {0: -h01 * v0[0] - h11 * v1[0], 1: image[1] - h11 * v1[1], 2: image[2]}
    h21 = jnp.sqrt(form(image, image))

    radius = jnp.full(totals.shape, radius_ref[0], jnp.float32)
    ridge = 1.0 / (radius * radius)
    n00 = h00 * h00 + h10 * h10 + ridge
    n01 = h00 * h01 + h10 * h11
    n11 = h01 * h01 + h11 * h11 + h21 * h21 + ridge
    f00 = jnp.sqrt(n00)
    f10 = n01 / f00
    f11 = jnp.sqrt(n11 - f10 * f10)
    r0 = norm * h00 / f00
    r1 = (norm * h01 - f10 * r0) / f11
    w1 = r1 / f11
    w0 = (r0 - f10 * w1) / f00
    m0 = w0 * v0[0] + w1 * v1[0]
    m1 = w1 * v1[1]

    shape = hess_ref.shape
    i = lax.broadcasted_iota(jnp.int32, shape, 0)
    j = lax.broadcasted_iota(jnp.int32, shape, 1)
    hess = jnp.zeros(shape, jnp.float32)
    for r, c, value in ((0, 0, h00), (1, 0, h10), (0, 1, h01), (1, 1, h11), (2, 1, h21)):
        hess = jnp.where((i == r) & (j == c), value[:, : shape[1]], hess)
    hess_ref[...] = hess

    stores = []
    for n, piece in enumerate(pieces):
        for load in loads[n]:
            load.wait()
        y[piece] = m0 * x0[piece] + m1 * x1[piece]
        store = pltpu.make_async_copy(y.at[piece], step_ref.at[piece], out_sem.at[n])
        store.start()
        stores.append(store)
    for store in stores:
        store.wait()


def local(seg_n, slab_n, mismatch, advect, damping, axial_shift, radius):
    one, loc, rows, lanes = mismatch.shape
    shape = (loc, rows // 8, 8, lanes)
    width = WIDTH
    full = loc + 2 * width
    p, a, g = (x.reshape(shape) for x in (mismatch, advect, damping))
    plane = shape[1:]
    exchanges = KRY * STEPS // width
    dma = pltpu.SemaphoreType.DMA
    anywhere = pl.BlockSpec(memory_space=pl.ANY)
    smem = pl.BlockSpec(memory_space=pltpu.SMEM)
    vmem = pl.BlockSpec(memory_space=pltpu.VMEM)
    f32 = jnp.float32
    p1, totals = pl.pallas_call(
        functools.partial(krylov_kernel, seg_n, slab_n, width),
        out_shape=(jax.ShapeDtypeStruct(shape, f32), jax.ShapeDtypeStruct((1, lanes), f32)),
        in_specs=[smem, anywhere, anywhere, anywhere],
        out_specs=(anywhere, vmem),
        scratch_shapes=[
            pltpu.VMEM((KRY * STEPS + 1, full) + plane, f32),
            pltpu.VMEM((full,) + plane, f32),
            pltpu.VMEM((full,) + plane, f32),
            pltpu.VMEM((2 * loc,) + plane, f32),
            pltpu.VMEM((2 * loc,) + plane, f32),
            pltpu.VMEM((seg_n, 1, lanes), f32),
            pltpu.VMEM((slab_n, 1, lanes), f32),
            dma((3,)),
            dma((exchanges + 2, 2)),
            dma((exchanges + 2, 2)),
            dma((KRY,)),
            dma((KRY,)),
            dma((KRY,)),
            dma((KRY,)),
            dma,
            dma((seg_n - 1,)),
            dma((seg_n - 1,)),
            dma((slab_n - 1,)),
            dma((slab_n - 1,)),
        ],
        compiler_params=pltpu.CompilerParams(
            collective_id=0, has_side_effects=True, vmem_limit_bytes=32 * 2**20
        ),
        name="krylov",
    )(axial_shift, p, a, g)
    step, hessenberg = pl.pallas_call(
        step_kernel,
        out_shape=(jax.ShapeDtypeStruct(shape, f32), jax.ShapeDtypeStruct((KRY + 1, KRY), f32)),
        in_specs=[smem, vmem, anywhere, anywhere],
        out_specs=(anywhere, vmem),
        scratch_shapes=[
            pltpu.VMEM(shape, f32),
            pltpu.VMEM(shape, f32),
            pltpu.VMEM(shape, f32),
            dma((2, 4)),
            dma((4,)),
        ],
        compiler_params=pltpu.CompilerParams(vmem_limit_bytes=16 * 2**20),
        name="hookstep",
    )(radius, totals, p, p1)
    return step.reshape(mismatch.shape), hessenberg


def solution(mesh):
    field = P("seg", "slab", None, None)
    return jax.shard_map(
        functools.partial(local, mesh.shape["seg"], mesh.shape["slab"]),
        mesh=mesh,
        in_specs=(field, field, field, P(), P()),
        out_specs=(field, P()),
        check_vma=False,
    )
```

```python
import functools

import jax
import jax.numpy as jnp
from jax import lax
from jax.experimental import pallas as pl
from jax.experimental.pallas import tpu as pltpu
from jax.sharding import PartitionSpec as P

STEPS = 8
KRY = 2
KAPPA = 0.15
WIDTH = 4

MESH = pl.DeviceIdType.MESH


def rows_of(ref, *place):
    groups = ref.shape[-2] // 8
    return [ref[(*place, pl.ds(j, 8, groups))] for j in range(groups)]


def stencil(behind, centre, ahead, drift, keep):
    groups = len(centre)
    lanes = centre[0].shape[-1]
    row = lax.broadcasted_iota(jnp.int32, centre[0].shape, 0)
    inner = [jnp.where(row == 0, 0.0, pltpu.roll(centre[-1], 1, 0))] + centre[:-1]
    outer = centre[1:] + [jnp.where(row == 7, 0.0, pltpu.roll(centre[0], 7, 0))]
    result = []
    for j in range(groups):
        around = pltpu.roll(centre[j], 1, 1) + pltpu.roll(centre[j], lanes - 1, 1)
        total = (around + (inner[j] + outer[j])) + (ahead[j] + behind[j])
        result.append(centre[j] * keep[j] + KAPPA * total + drift[j] * (behind[j] - ahead[j]))
    return result


def krylov_kernel(
    seg_n, slab_n, width,
    shift_ref, p_ref, a_ref, g_ref,
    p1_ref, totals_ref,
    levels, adv, dam, next_a, next_b, relay, seg_sums, slab_sums,
    load_sem, halo_send, halo_recv, pair_send, pair_recv, cross_send, cross_recv,
    out_sem, seg_send, seg_recv, slab_send, slab_recv,
):
    loc = p_ref.shape[0]
    full = loc + 2 * width
    half = loc // 2
    seg = lax.axis_index("seg")
    slab = lax.axis_index("slab")
    at = lambda s, z: {"seg": lax.rem(seg + s, seg_n), "slab": lax.rem(slab + z, slab_n)}
    coupled = (next_a, next_b)

    barrier = pltpu.get_barrier_semaphore()
    peers = [(0, z) for z in range(1, slab_n)] + [(s, 0) for s in range(1, seg_n)]
    for s, z in peers:
        pl.semaphore_signal(barrier, inc=1, device_id=at(s, z), device_id_type=MESH)
    own = pl.ds(width, loc)
    loads = [
        pltpu.make_async_copy(p_ref, levels.at[0, own], load_sem.at[0]),
        pltpu.make_async_copy(a_ref, adv.at[own], load_sem.at[1]),
        pltpu.make_async_copy(g_ref, dam.at[own], load_sem.at[2]),
    ]
    for load in loads:
        load.start()

    def halo(source, first, target, count, place):
        return [
            pltpu.make_async_remote_copy(
                src_ref=source.at[pl.ds(first + loc - count, count)],
                dst_ref=target.at[pl.ds(width - count, count)],
                send_sem=halo_send.at[place, 0], recv_sem=halo_recv.at[place, 0],
                device_id=at(0, 1), device_id_type=MESH,
            ),
            pltpu.make_async_remote_copy(
                src_ref=source.at[pl.ds(first, count)],
                dst_ref=target.at[pl.ds(width + loc, count)],
                send_sem=halo_send.at[place, 1], recv_sem=halo_recv.at[place, 1],
                device_id=at(0, slab_n - 1), device_id_type=MESH,
            ),
        ]

    def pair(source, column):
        return [
            pltpu.make_async_remote_copy(
                src_ref=source.at[pl.ds(part * half, half)],
                dst_ref=coupled[column].at[pl.ds(loc + part * half, half)],
                send_sem=pair_send.at[column, part], recv_sem=pair_recv.at[column, part],
                device_id=at(seg_n - 1, 0), device_id_type=MESH,
            )
            for part in (1, 0)
        ]

    def behind_first(source, column):
        return pltpu.make_async_remote_copy(
            src_ref=source.at[pl.ds(0, half)], dst_ref=relay.at[column],
            send_sem=cross_send.at[column, 0], recv_sem=cross_recv.at[column, 0],
            device_id=at(0, 1), device_id_type=MESH,
        )

    def first_to_last(column):
        return pltpu.make_async_remote_copy(
            src_ref=relay.at[column], dst_ref=coupled[column].at[pl.ds(0, half)],
            send_sem=cross_send.at[column, 1], recv_sem=cross_recv.at[column, 1],
            device_id=at(seg_n - 1, 0), device_id_type=MESH,
        )

    def behind_last(column):
        return pltpu.make_async_remote_copy(
            src_ref=coupled[column].at[pl.ds(loc + half, half)],
            dst_ref=coupled[column].at[pl.ds(half, half)],
            send_sem=cross_send.at[column, 2], recv_sem=cross_recv.at[column, 2],
            device_id=at(0, 1), device_id_type=MESH,
        )

    def couple_start(source, column):
        for copy in pair(source, column):
            copy.start()

        @pl.when(seg == 0)
        def _():
            behind_first(source, column).start()

    def couple_relay(source, column):
        @pl.when(seg == 0)
        def _():
            behind_first(source, column).wait()
            first_to_last(column).start()

        @pl.when(seg == seg_n - 1)
        def _():
            pair(source, column)[0].wait_recv()
            behind_last(column).start()

    def couple_wait(source, column):
        high, low = pair(source, column)
        high.wait_send()
        low.wait()

        @pl.when(seg < seg_n - 1)
        def _():
            high.wait_recv()

        @pl.when(seg == 0)
        def _():
            first_to_last(column).wait_send()

        @pl.when(seg == seg_n - 1)
        def _():
            first_to_last(column).wait_recv()
            behind_last(column).wait()

    def sweep(level, start, count):
        groups = levels.shape[-2] // 8
        before = rows_of(levels, level, start - 1)
        here = rows_of(levels, level, start)
        for plane in range(count):
            after = rows_of(levels, level, start + plane + 1)
            result = stencil(
                before, here, after, rows_of(adv, start + plane), rows_of(dam, start + plane)
            )
            for j in range(groups):
                levels[level + 1, start + plane, pl.ds(j, 8, groups)] = result[j]
            before, here = here, after

    def prepare(start, count):
        for plane in range(count):
            adv[start + plane] = 0.5 * adv[start + plane]
            dam[start + plane] = (1.0 - 6.0 * KAPPA) - dam[start + plane]

    thirds = -(-(loc - 2) // 3)

    def interior(base):
        def one(k, carry):
            def piece(i, inner):
                sweep(base + k, width + k + 1 + (i * (loc - 2 - 2 * k - thirds)) // 2, thirds)
                return inner
            return lax.fori_loop(0, 3, piece, carry)
        lax.fori_loop(0, width, one, 0)

    def edges(base):
        def one(k, carry):
            sweep(base + k, k + 1, width)
            sweep(base + k, full - 1 - k - width, width)
            return carry
        lax.fori_loop(0, width, one, 0)

    pl.semaphore_wait(barrier, len(peers))
    exchanges = KRY * STEPS // width
    sent = halo(p_ref, 0, levels.at[0], width, 0)
    sent += halo(a_ref, 0, adv, width - 1, exchanges)
    sent += halo(g_ref, 0, dam, width - 1, exchanges + 1)
    for copy in sent:
        copy.start()
    couple_start(p_ref, 0)

    for load in loads:
        load.wait()

    def prepare_group(i, carry):
        prepare(width + 4 * i, 4)
        return carry

    lax.fori_loop(0, loc // 4, prepare_group, 0)
    zero = jnp.zeros(p_ref.shape[1:], jnp.float32)
    offset = jnp.where(seg == seg_n - 1, loc - shift_ref[0], loc)
    sums = []
    for column in range(KRY):
        source = p_ref if column == 0 else levels.at[STEPS, own]
        for part in range(STEPS // width):
            base = column * STEPS + part * width
            if base > 0:
                sent = halo(levels.at[base], width, levels.at[base], width, base // width)
                for copy in sent:
                    copy.start()
                if part == 0:
                    couple_start(source, column)
            if part == 1:
                couple_relay(source, column)
            interior(base)
            for copy in sent:
                copy.wait()
            if base == 0:
                prepare(1, width - 1)
                prepare(width + loc, width - 1)
            edges(base)
        couple_wait(source, column)
        last = (column + 1) * STEPS

        def couple(i, acc):
            image = levels[last, width + i] - coupled[column][offset + i]
            if column == 0:
                levels[last, width + i] = image
            first = levels[0, width + i]
            second = image if column == 0 else levels[STEPS, width + i]
            head = first * first if column == 0 else first * image
            mid = first * image if column == 0 else second * image
            return (acc[0] + head, acc[1] + mid, acc[2] + image * image)

        def couple_group(i, acc):
            for j in range(4):
                acc = couple(4 * i + j, acc)
            return acc

        sums += lax.fori_loop(0, loc // 4, couple_group, (zero, zero, zero))
        if column == 0:
            store = pltpu.make_async_copy(levels.at[STEPS, own], p1_ref, out_sem)
            store.start()

    lane = lax.broadcasted_iota(jnp.int32, (1, zero.shape[-1]), 1)
    row = jnp.zeros(lane.shape, jnp.float32)
    for place, entry in enumerate(sums):
        value = jnp.sum(entry, axis=(0, 1), keepdims=True)
        row = row + jnp.where(lane == place, value, 0.0)

    def share(row, buffer, me, count, where, send, recv):
        buffer[me] = row
        copies = []
        for d in range(1, count):
            copies.append(
                pltpu.make_async_remote_copy(
                    src_ref=buffer.at[me], dst_ref=buffer.at[me],
                    send_sem=send.at[d - 1], recv_sem=recv.at[d - 1],
                    device_id=where(d), device_id_type=MESH,
                )
            )
        for copy in copies:
            copy.start()
        for copy in copies:
            copy.wait()
        total = buffer[0]
        for d in range(1, count):
            total = total + buffer[d]
        return total

    row = share(row, seg_sums, seg, seg_n, lambda d: at(d, 0), seg_send, seg_recv)
    row = share(row, slab_sums, slab, slab_n, lambda d: at(0, d), slab_send, slab_recv)
    totals_ref[...] = row
    store.wait()


def step_kernel(radius_ref, totals_ref, p0_ref, p1_ref, step_ref, hess_ref, x0, x1, y, in_sem, out_sem):
    loc = p0_ref.shape[0]
    parts = 4
    size = loc // parts
    pieces = [pl.ds(i * size, size) for i in range(parts)]
    loads = []
    for i, piece in enumerate(pieces):
        loads.append(
            (
                pltpu.make_async_copy(p0_ref.at[piece], x0.at[piece], in_sem.at[0, i]),
                pltpu.make_async_copy(p1_ref.at[piece], x1.at[piece], in_sem.at[1, i]),
            )
        )
    for pair in loads:
        for load in pair:
            load.start()

    totals = totals_ref[...]
    lane = lax.broadcasted_iota(jnp.int32, totals.shape, 1)
    entry = lambda i: jnp.sum(jnp.where(lane == i, totals, 0.0), axis=1, keepdims=True)
    g00, g01, g11, g02, g12, g22 = [jnp.broadcast_to(entry(i), totals.shape) for i in range(6)]
    gram = ((g00, g01, g02), (g01, g11, g12), (g02, g12, g22))

    def form(left, right):
        total = None
        for i, a in left.items():
            inner = None
            for j, b in right.items():
                term = gram[i][j] * b
                inner = term if inner is None else inner + term
            total = a * inner if total is None else total + a * inner
        return total

    norm = jnp.sqrt(g00)
    v0 = {0: 1.0 / norm}
    image = {1: v0[0]}
    h00 = form(v0, image)
    image = {0: -h00 * v0[0], 1: image[1]}
    h10 = jnp.sqrt(form(image, image))
    v1 = {0: image[0] / h10, 1: image[1] / h10}
    image = {1: v1[0], 2: v1[1]}
    h01 = form(v0, image)
    h11 = form(v1, image)
    image = {0: -h01 * v0[0] - h11 * v1[0], 1: image[1] - h11 * v1[1], 2: image[2]}
    h21 = jnp.sqrt(form(image, image))

    radius = jnp.full(totals.shape, radius_ref[0], jnp.float32)
    ridge = 1.0 / (radius * radius)
    n00 = h00 * h00 + h10 * h10 + ridge
    n01 = h00 * h01 + h10 * h11
    n11 = h01 * h01 + h11 * h11 + h21 * h21 + ridge
    f00 = jnp.sqrt(n00)
    f10 = n01 / f00
    f11 = jnp.sqrt(n11 - f10 * f10)
    r0 = norm * h00 / f00
    r1 = (norm * h01 - f10 * r0) / f11
    w1 = r1 / f11
    w0 = (r0 - f10 * w1) / f00
    m0 = w0 * v0[0] + w1 * v1[0]
    m1 = w1 * v1[1]

    shape = hess_ref.shape
    i = lax.broadcasted_iota(jnp.int32, shape, 1)
    j = lax.broadcasted_iota(jnp.int32, shape, 0)
    hess = jnp.zeros(shape, jnp.float32)
    for r, c, value in ((0, 0, h00), (1, 0, h10), (0, 1, h01), (1, 1, h11), (2, 1, h21)):
        hess = jnp.where((i == r) & (j == c), value[:, : shape[1]], hess)
    hess_ref[...] = hess

    stores = []
    for n, piece in enumerate(pieces):
        for load in loads[n]:
            load.wait()
        y[piece] = m0 * x0[piece] + m1 * x1[piece]
        store = pltpu.make_async_copy(y.at[piece], step_ref.at[piece], out_sem.at[n])
        store.start()
        stores.append(store)
    for store in stores:
        store.wait()


def local(seg_n, slab_n, mismatch, advect, damping, axial_shift, radius):
    one, loc, rows, lanes = mismatch.shape
    shape = (loc, rows, lanes)
    width = WIDTH
    full = loc + 2 * width
    p, a, g = (x.reshape(shape) for x in (mismatch, advect, damping))
    plane = shape[1:]
    exchanges = KRY * STEPS // width
    dma = pltpu.SemaphoreType.DMA
    anywhere = pl.BlockSpec(memory_space=pl.ANY)
    smem = pl.BlockSpec(memory_space=pltpu.SMEM)
    vmem = pl.BlockSpec(memory_space=pltpu.VMEM)
    f32 = jnp.float32
    p1, totals = pl.pallas_call(
        functools.partial(krylov_kernel, seg_n, slab_n, width),
        out_shape=(jax.ShapeDtypeStruct(shape, f32), jax.ShapeDtypeStruct((1, lanes), f32)),
        in_specs=[smem, anywhere, anywhere, anywhere],
        out_specs=(anywhere, vmem),
        scratch_shapes=[
            pltpu.VMEM((KRY * STEPS + 1, full) + plane, f32),
            pltpu.VMEM((full,) + plane, f32),
            pltpu.VMEM((full,) + plane, f32),
            pltpu.VMEM((2 * loc,) + plane, f32),
            pltpu.VMEM((2 * loc,) + plane, f32),
            pltpu.VMEM((KRY, loc // 2) + plane, f32),
            pltpu.VMEM((seg_n, 1, lanes), f32),
            pltpu.VMEM((slab_n, 1, lanes), f32),
            dma((3,)),
            dma((exchanges + 2, 2)),
            dma((exchanges + 2, 2)),
            dma((KRY, 2)),
            dma((KRY, 2)),
            dma((KRY, 3)),
            dma((KRY, 3)),
            dma,
            dma((seg_n - 1,)),
            dma((seg_n - 1,)),
            dma((slab_n - 1,)),
            dma((slab_n - 1,)),
        ],
        compiler_params=pltpu.CompilerParams(
            collective_id=0, has_side_effects=True
        ),
        name="krylov",
    )(axial_shift, p, a, g)
    step, hessenberg = pl.pallas_call(
        step_kernel,
        out_shape=(jax.ShapeDtypeStruct(shape, f32), jax.ShapeDtypeStruct((KRY, KRY + 1), f32)),
        in_specs=[smem, vmem, anywhere, anywhere],
        out_specs=(anywhere, vmem),
        scratch_shapes=[
            pltpu.VMEM(shape, f32),
            pltpu.VMEM(shape, f32),
            pltpu.VMEM(shape, f32),
            dma((2, 4)),
            dma((4,)),
        ],
        name="hookstep",
    )(radius, totals, p, p1)
    return step.reshape(mismatch.shape), hessenberg.T


def solution(mesh):
    field = P("seg", "slab", None, None)
    return jax.shard_map(
        functools.partial(local, mesh.shape["seg"], mesh.shape["slab"]),
        mesh=mesh,
        in_specs=(field, field, field, P(), P()),
        out_specs=(field, P()),
        check_vma=False,
    )
```
